32 devices in a mesh: expert: 8 (over z, y), dp: 4 (over x, core).
Axes of the slice: x: 2, y: 2, z: 4, core: 2. Of those that a mesh axis runs over, the one named last changes fastest.
Arguments:
- tokens: bfloat16 [4096, 3584], P(('expert', 'dp')), may hold values from -6 to 6
- cotangent: bfloat16 [4096, 3584], P(('expert', 'dp')), may hold values from -6 to 6
- routes: int32 [4096, 1], P(('expert', 'dp')), may hold values from 0 to 1; in each aligned block of 128 rows (0 to 127, 128 to 255, ...) at most 80 rows name the same one
- gates: bfloat16 [4096, 1], P(('expert', 'dp')), may hold values from 0.049804688 to 1
- w_gate: bfloat16 [2048, 3584], P('expert', 'dp'), may hold values from -0.09375 to 0.09375
- w_up: bfloat16 [2048, 3584], P('expert', 'dp'), may hold values from -0.09375 to 0.09375
- w_down: bfloat16 [2048, 3584], P('expert', 'dp'), may hold values from -0.1875 to 0.1875
Outputs:
- grad_up: bfloat16 [2048, 3584], P('expert', 'dp')
- grad_down: bfloat16 [2048, 3584], P('expert', 'dp')
- grad_gates: float32 [4096, 1], P(('expert', 'dp'))
The draws below stay inside these ranges and needn't reach their ends.
Inputs may be any that keep to these rules, and one draw needn't show every extreme that they name: `routes`: the 1 entries of a row are distinct. Among the 128 rows of one device, no expert is named more than 80 times, a bound that some block reaches.
All inputs are finite; a program needn't handle non-finite values.
Results may differ from the reference program's by a relative error of at most 0.009.
Values may be sent and summed in bfloat16 or wider, within the bound.
A program may use at most 128 MiB of HBM per device.

```python
import math
import jax
import jax.numpy as jnp
import numpy as np
from jax import lax

D = 3584
FF = 1024
TOP = 1
TOK_DEV = 128
EXPERTS = 2
CAP = 80
TOKENS = 4096
N_EXPERT = 8
N_DP = 4


def block_scale(own_key, shape, split, low, top_value):
    loudness = 1.0
    for axis_at, blocks in split:
        heights = jax.random.uniform(jax.random.fold_in(jax.random.fold_in(own_key, 6), axis_at), (blocks,), jnp.float32, low / len(split), top_value / len(split))
        loudness = loudness * jnp.repeat(jnp.exp(heights), shape[axis_at] // blocks).reshape((-1,) + (1,) * (len(shape) - 1 - axis_at))
    return loudness


def deal_out(stream_key, own, number, rows, count, top, most, slope):
    order = jax.random.permutation(stream_key, count)
    crowded, usual = load_shares(count, rows * top, most, slope, True), load_shares(count, rows * top, most, slope, False)
    places = jnp.arange(count)

    def named(sizes, offset_by):
        used = int((sizes > 0).sum())
        fixed = max(1, used // 4)
        moved = fixed + (places - fixed + offset_by * (used - fixed)) % max(1, count - fixed)
        return jnp.zeros((count,), jnp.int32).at[order[jnp.where(places < fixed, places, moved)]].set(jnp.asarray(sizes, jnp.int32))

    sizes = jnp.where(number % 4 == 0, named(crowded, number // 4), named(usual, number - number // 4 - 1))
    mixed = jax.random.permutation(jax.random.fold_in(own, 3), count)
    donor, receiver = mixed[0:count // 2 * 2:2], mixed[1:count // 2 * 2:2]
    slack = jnp.minimum(sizes[donor] - 1, most - sizes[receiver]) // 2
    slack = jnp.where((donor == order[0]) | (receiver == order[0]) | (sizes[receiver] == 0), 0, jnp.maximum(slack, 0))
    moved = jax.random.randint(jax.random.fold_in(own, 4), (count // 2,), 0, 1 << 20) % (slack + 1)
    sizes = sizes.at[donor].add(-moved).at[receiver].add(moved)
    items = jnp.searchsorted(jnp.cumsum(sizes), jnp.arange(rows * top), side="right").astype(jnp.int32)
    listing = items.reshape(top, rows).T
    listing = listing[jax.random.permutation(jax.random.fold_in(own, 1), rows)]
    offset_by = jax.random.randint(jax.random.fold_in(own, 2), (rows, 1), 0, top)
    return jnp.take_along_axis(listing, (jnp.arange(top)[None, :] + offset_by) % top, axis=1)


def load_shares(amount, total, reach, slope, full):
    portions = [(1 << 20) // math.isqrt(grade ** slope) + 1 for grade in range(1, amount + 1)]
    largest = reach if full else min(reach, max(-(-total // amount), total * portions[0] // sum(portions)))
    least = 1 if total - largest >= amount - 1 else 0
    counts, rest = [largest] + [least] * (amount - 1), total - largest - least * (amount - 1)
    while rest > 0:
        candidates = [i for i in range(1, amount) if counts[i] < largest] or [i for i in range(1, amount) if counts[i] < reach]
        pool, remaining = sum([portions[i] for i in candidates]), rest
        for i in candidates:
            addition = min(reach - counts[i], max(1, remaining * portions[i] // pool), rest)
            counts[i] = counts[i] + addition
            rest = rest - addition
    return np.array(counts)


def bell_draw(own_key, extent, deviation, bound, split=(), kind=jnp.bfloat16):
    values = jax.random.normal(own_key, extent, jnp.float32) * deviation
    if len(split) > 0:
        values = block_scale(own_key, extent, split, -0.22, 0.18) * values
    return jnp.clip(values, min=-bound, max=bound).astype(kind)


def setup_inputs(seed: int = 0) -> dict:
    arg_keys = jax.random.split(jax.random.key(seed), 8)
    tokens = bell_draw(arg_keys[0], (TOKENS, D), 1.0, 6.0, ((0, 32),))
    cotangent = bell_draw(arg_keys[1], (TOKENS, D), 1.0, 6.0, ((0, 32),))
    routes_keys = jax.random.split(jax.random.fold_in(arg_keys[2], 1), TOKENS // TOK_DEV)
    routes_turns = jax.random.permutation(jax.random.fold_in(arg_keys[2], 3), TOKENS // TOK_DEV)
    routes = jax.vmap(lambda own, number: deal_out(jax.random.fold_in(arg_keys[2], 2), own, number, TOK_DEV, EXPERTS, TOP, CAP, 1))(routes_keys, routes_turns).reshape((TOKENS, TOP))
    gates = jnp.clip(jnp.exp(math.log(1.0) - 2.9996462 * jax.random.uniform(arg_keys[3], (TOKENS, TOP), jnp.float32) ** block_scale(arg_keys[3], (TOKENS, TOP), ((0, 32),), -0.2, 0.2)), 0.049804688, 1.0).astype(jnp.bfloat16)
    w_gate = bell_draw(arg_keys[4], (EXPERTS * FF, D), D ** -0.5, 0.09375, ((0, 8), (1, 4)))
    w_up = bell_draw(arg_keys[5], (EXPERTS * FF, D), D ** -0.5, 0.09375, ((0, 8), (1, 4)))
    w_down = bell_draw(arg_keys[6], (EXPERTS * FF, D), FF ** -0.5, 0.1875, ((0, 8), (1, 4)))
    return dict(tokens=tokens, cotangent=cotangent, routes=routes, gates=gates, w_gate=w_gate, w_up=w_up, w_down=w_down)


def reference(tokens, cotangent, routes, gates, w_gate, w_up, w_down):
    total = tokens.shape[0]
    experts = w_gate.shape[0] // FF
    pairs = total * TOP
    limit = N_DP * N_EXPERT * CAP
    flat_routes = routes.reshape(-1)
    flat_gates = gates.reshape(-1)

    def one_expert(expert_id):
        mask = flat_routes == expert_id
        order = jnp.cumsum(mask.astype(jnp.int32)) - 1
        target = jnp.where(mask, order, limit).astype(jnp.int32)
        picked = jnp.zeros((limit,), jnp.int32).at[target].set(jnp.arange(pairs, dtype=jnp.int32), mode="drop")
        count = jnp.sum(mask.astype(jnp.int32))
        valid = jnp.arange(limit, dtype=jnp.int32) < count
        tok_index = picked // TOP
        rows_x = jnp.where(valid[:, None], tokens[tok_index], jnp.zeros((), jnp.bfloat16))
        rows_dy = jnp.where(valid[:, None], cotangent[tok_index], jnp.zeros((), jnp.bfloat16))
        weight = jnp.where(valid, flat_gates[picked].astype(jnp.float32), jnp.float32(0.0))
        start = (expert_id * FF).astype(jnp.int32)
        wg = lax.dynamic_slice_in_dim(w_gate, start, FF, 0)
        wu = lax.dynamic_slice_in_dim(w_up, start, FF, 0)
        wd = lax.dynamic_slice_in_dim(w_down, start, FF, 0)
        pre_a = jnp.dot(rows_x, wg.T, preferred_element_type=jnp.float32)
        pre_b = jnp.dot(rows_x, wu.T, preferred_element_type=jnp.float32)
        sig = jax.nn.sigmoid(pre_a)
        silu = pre_a * sig
        hidden = (silu * pre_b).astype(jnp.bfloat16)
        probe = jnp.dot(rows_dy, wd.T, preferred_element_type=jnp.float32)
        gate_grad = jnp.sum(hidden.astype(jnp.float32) * probe, axis=1)
        scaled = (weight[:, None] * rows_dy.astype(jnp.float32)).astype(jnp.bfloat16)
        d_b = (weight[:, None] * probe * silu).astype(jnp.bfloat16)
        replica = (tok_index // TOK_DEV) % N_DP
        sum_up = jnp.zeros((FF, D), jnp.float32)
        sum_down = jnp.zeros((FF, D), jnp.float32)
        zero_b = jnp.zeros((), jnp.bfloat16)
        for rep in range(N_DP):
            select = (valid & (replica == rep))[:, None]
            part_b = jnp.where(select, d_b, zero_b)
            part_h = jnp.where(select, hidden, zero_b)
            sum_up = sum_up + jnp.dot(part_b.T, rows_x, preferred_element_type=jnp.float32).astype(jnp.bfloat16).astype(jnp.float32)
            sum_down = sum_down + jnp.dot(part_h.T, scaled, preferred_element_type=jnp.float32).astype(jnp.bfloat16).astype(jnp.float32)
        where_back = jnp.where(valid, picked, pairs).astype(jnp.int32)
        return (sum_up.astype(jnp.bfloat16), sum_down.astype(jnp.bfloat16), gate_grad, where_back)

    grad_u, grad_d, gate_rows, where_all = lax.map(one_expert, jnp.arange(experts, dtype=jnp.int32))
    flat_grad = jnp.zeros((pairs,), jnp.float32).at[where_all.reshape(-1)].add(gate_rows.reshape(-1), mode="drop")
    return (grad_u.reshape(experts * FF, D), grad_d.reshape(experts * FF, D), flat_grad.reshape(total, TOP))
```

```python
import jax
import jax.numpy as jnp
from jax import lax
from jax.experimental import pallas as pl
from jax.experimental.pallas import tpu as pltpu
from jax.sharding import PartitionSpec as P

SPLIT = 4
TOP = 1
TOK_DEV = 128
MESH = pl.DeviceIdType.MESH
ORDER = (0, 4, 1, 5)
PLACE = {c: i for i, c in enumerate(ORDER)}
PIECE = 256


def flip(index, code):
    for bit in (1, 2, 4):
        if code & bit:
            index = index + bit - 2 * bit * ((index // bit) % 2)
    return index


def fused_kernel(
    cap, oh_ref, ohg_ref, tok_ref, cot_ref, wg_ref, wu_ref, wd_ref,
    up_ref, down_ref, share_ref,
    rows_x, rows_c, near, far, w_all, t_sum, core_out, core_in, x_out, x_in, t_h, t_d,
    own, z_out, z_in, share_mine, share_all,
    local_sem, row_send, row_recv, w_send, w_recv, core_send, core_recv, x_send, x_recv,
    act_send, act_recv, z_send, z_recv, share_send, share_recv,
):
    e = lax.axis_index("expert")
    d = lax.axis_index("dp")
    hidden, cols = wg_ref.shape
    half = t_sum.shape[2]
    per = hidden // PIECE
    nt = (((1,), (1,)), ((), ()))
    nn = (((1,), (0,)), ((), ()))
    f32, bf16 = jnp.float32, jnp.bfloat16
    x_here = d // 2
    x_there = 1 - x_here

    def at_device(code, rel):
        return {"expert": flip(e, code), "dp": flip(d, rel)}

    barrier = pltpu.get_barrier_semaphore()
    peers = ((0, 1), (0, 2), (0, 3), (1, 0), (2, 0), (4, 0), (4, 1), (4, 2), (4, 3), (5, 0))
    for code, rel in peers:
        pl.semaphore_signal(barrier, inc=1, device_id=at_device(code, rel), device_id_type=MESH)
    pl.semaphore_wait(barrier, len(peers))

    sent = []

    def push(src, dst, send_sem, recv_sem, device):
        copy = pltpu.make_async_remote_copy(
            src_ref=src, dst_ref=dst, send_sem=send_sem, recv_sem=recv_sem,
            device_id=device, device_id_type=MESH,
        )
        copy.start()
        sent.append(copy)
        return copy

    rows = (rows_x, rows_c)
    whole = (tok_ref, cot_ref)
    hots = (oh_ref, ohg_ref)

    def block(kind, rel, source_x, code):
        number = (rel % 2) * 8 + source_x * 4 + PLACE[code]
        return rows[kind].at[pl.ds(pl.multiple_of(number * cap, 16), cap), :]

    def pick(kind, low, rel):
        lanes = pl.ds(pl.multiple_of(flip(d, rel) * cols, 128), cols)
        return lax.dot_general(
            hots[kind][low : low + cap, :], whole[kind][:, lanes], nn, preferred_element_type=f32
        ).astype(bf16)

    row_copy = {}

    def send_block(kind, code, rel, source, there, source_x, device):
        row_copy[kind, code, rel] = push(
            source, there, row_send.at[kind, PLACE[code], rel], row_recv.at[kind, PLACE[code], rel], device
        )

    def send_far(kind, rel):
        far[kind, rel] = pick(kind, cap, rel)
        send_block(kind, 4, rel, far.at[kind, rel], block(kind, rel, x_here, 4), x_here, at_device(4, rel))

    def send_near(kind, rel):
        if rel == 0:
            mine = block(kind, 0, x_here, 0)
            mine[...] = pick(kind, 0, 0)
            pass_on(kind, 0, 0)
        else:
            near[kind, rel - 1] = pick(kind, 0, rel)
            send_block(
                kind, 0, rel, near.at[kind, rel - 1], block(kind, rel, x_here, 0), x_here, at_device(0, rel)
            )

    def pass_on(kind, code, rel):
        source_x = x_there if rel // 2 else x_here
        send_block(
            kind, code + 1, rel, block(kind, rel, source_x, code), block(kind, rel, source_x, code + 1),
            source_x, at_device(1, 0),
        )

    def got(kind, code, rel):
        row_copy[kind, code, rel].wait_recv()

    def forward(kind, code, rel):
        got(kind, code, rel)
        pass_on(kind, code, rel)

    w_in = (wg_ref, wu_ref, wd_ref)
    w_copy = {}
    local = {}

    def w_own(k):
        w_copy[k] = push(
            w_in[k], w_all.at[k, hidden : 2 * hidden], w_send.at[k], w_recv.at[k], at_device(2, 0)
        )

    def w_keep(k):
        local[k] = pltpu.make_async_copy(w_in[k], w_all.at[k, 0:hidden], local_sem.at[k])
        local[k].start()

    def span(q):
        return slice(q * PIECE, (q + 1) * PIECE)

    core_copy = {}
    x_copy = {}
    act_copy = {}
    z_copy = {}

    def project(k, q):
        out = lax.dot_general(
            w_all[k, span(q), :], rows[k // 2][...], nt, preferred_element_type=f32
        )
        core_out[k, span(q), :] = out[:, half:]
        core_copy[k, q] = push(
            core_out.at[k, span(q)], core_in.at[k, span(q)],
            core_send.at[k, q], core_recv.at[k, q], at_device(0, 1),
        )
        t_sum[k, span(q), :] = out[:, :half]

    def cross(k, q):
        core_copy[k, q].wait_recv()
        both = t_sum[k, span(q), :] + core_in[k, span(q), :]
        x_out[k, span(q), :] = both.astype(bf16)
        x_copy[k, q] = push(
            x_out.at[k, span(q)], x_in.at[k, span(q)], x_send.at[k, q], x_recv.at[k, q], at_device(0, 2)
        )
        t_sum[k, span(q), :] = both

    def total(k, q):
        x_copy[k, q].wait_recv()
        return t_sum[k, span(q), :] + x_in[k, span(q), :].astype(f32)

    def hand_over(g, ref, q):
        act_copy[g, q] = push(
            ref.at[span(q), 0:half], ref.at[span(q), half : 2 * half],
            act_send.at[g, q], act_recv.at[g, q], at_device(0, 1),
        )

    def activate(q):
        a = total(0, q)
        silu = a * jax.nn.sigmoid(a)
        t_h[span(q), 0:half] = (silu * total(1, q)).astype(bf16)
        hand_over(1, t_h, q)
        t_sum[0, span(q), :] = silu

    def derive(q):
        p = total(2, q)
        t_d[span(q), 0:half] = (p * t_sum[0, span(q), :]).astype(bf16)
        hand_over(0, t_d, q)
        t_sum[2, span(q), :] = p

    left = (t_d, t_h)

    def gradient(g, q):
        act_copy[g, q].wait_recv()
        out = lax.dot_general(
            left[g][span(q), :], rows[g][...], nn, preferred_element_type=f32
        )
        if q < per:
            own[g, span(q), :] = out
        else:
            there = span(q - per)
            z_out[g, there, :] = out.astype(bf16)
            z_copy[g, q - per] = push(
                z_out.at[g, there], z_in.at[g, there],
                z_send.at[g, q - per], z_recv.at[g, q - per], at_device(2, 0),
            )

    mine_q = tuple(range(per))
    their_q = tuple(range(per, 2 * per))

    for rel in (2, 0, 3, 1):
        send_far(0, rel)
    for rel in (0, 2, 3, 1):
        send_near(0, rel)
    for k in (0, 1):
        w_own(k)
    for k in (0, 1, 2):
        w_keep(k)
    for rel in (2, 0, 3, 1):
        send_far(1, rel)
    for rel in (2, 3, 1):
        send_near(1, rel)
    w_own(2)
    for rel in (1, 2, 3):
        forward(0, 0, rel)
    for rel in (0, 1, 2, 3):
        forward(0, 4, rel)
    send_near(1, 0)
    for rel in (1, 2, 3):
        forward(1, 0, rel)
    for code in (1, 5):
        for rel in (0, 1, 2, 3):
            got(0, code, rel)
    for k in (0, 1):
        local[k].wait()
        for q in mine_q:
            project(k, q)
    for k in (0, 1):
        for q in mine_q:
            cross(k, q)
    for rel in (0, 1):
        forward(1, 4, rel)
    for k in (0, 1):
        w_copy[k].wait_recv()
        for q in their_q:
            project(k, q)
    for k in (0, 1):
        for q in their_q:
            cross(k, q)
    for rel in (2, 3):
        forward(1, 4, rel)
    for q in mine_q:
        activate(q)
    for code in (1, 5):
        for rel in (0, 1, 2, 3):
            got(1, code, rel)
    w_copy[2].wait_recv()
    for q in their_q:
        project(2, q)
    local[2].wait()
    for q in their_q:
        cross(2, q)
    for q in mine_q:
        project(2, q)
    for q in mine_q:
        cross(2, q)
    for q in their_q:
        activate(q)
    for q in their_q:
        gradient(1, q)
    for q in mine_q:
        gradient(1, q)
    for q in their_q:
        derive(q)
        gradient(0, q)
    for q in mine_q:
        derive(q)
    dots = jnp.sum(t_h[:, 0:half].astype(f32) * t_sum[2], axis=0, keepdims=True)
    share_mine[...] = jnp.broadcast_to(dots, share_mine.shape)
    share_copy = {}
    for code in (1, 4, 5):
        n = PLACE[code]
        share_copy[n] = push(
            share_mine, share_all.at[n], share_send.at[n], share_recv.at[n], at_device(code, 0)
        )
    share_ref[0:1, :] = share_mine[0:1, :]
    for q in mine_q:
        gradient(0, q)
    for g, out in ((1, down_ref), (0, up_ref)):
        for q in mine_q:
            z_copy[g, q].wait_recv()
            out[span(q), :] = (own[g, span(q), :] + z_in[g, span(q), :].astype(f32)).astype(bf16)
    for n in (1, 2, 3):
        share_copy[n].wait_recv()
        share_ref[n : n + 1, :] = share_all[n, 0:1, :]
    for copy in sent:
        copy.wait_send()


def fused(cap, tokens, cotangent, routes, gates, w_gate, w_up, w_down):
    near = lax.axis_index("expert") // SPLIT
    flat, slot = slot_of(routes, 2)
    ids = jnp.arange(2 * cap, dtype=jnp.int32)
    named = jnp.where(ids < cap, near, 1 - near)
    placed = (flat[None, :] == named[:, None]) & (slot[None, :] == (ids % cap)[:, None])
    hot = placed.astype(jnp.bfloat16)
    weight = gates.reshape(-1)
    hot_gate = jnp.where(placed, weight[None, :], jnp.zeros((), jnp.bfloat16))
    hidden, cols = w_gate.shape
    half = 8 * cap
    per = hidden // PIECE
    bf16, f32 = jnp.bfloat16, jnp.float32
    vmem = pl.BlockSpec(memory_space=pltpu.VMEM)
    anywhere = pl.BlockSpec(memory_space=pl.ANY)
    dma = pltpu.SemaphoreType.DMA
    up, down, share = pl.pallas_call(
        lambda *refs: fused_kernel(cap, *refs),
        out_shape=(
            jax.ShapeDtypeStruct((hidden, cols), bf16),
            jax.ShapeDtypeStruct((hidden, cols), bf16),
            jax.ShapeDtypeStruct((4, half), f32),
        ),
        in_specs=[vmem] * 4 + [anywhere] * 3,
        out_specs=(vmem, vmem, vmem),
        scratch_shapes=[
            pltpu.VMEM((2 * half, cols), bf16),
            pltpu.VMEM((2 * half, cols), bf16),
            pltpu.VMEM((2, 3, cap, cols), bf16),
            pltpu.VMEM((2, 4, cap, cols), bf16),
            pltpu.VMEM((3, 2 * hidden, cols), bf16),
            pltpu.VMEM((3, 2 * hidden, half), f32),
            pltpu.VMEM((3, 2 * hidden, half), f32),
            pltpu.VMEM((3, 2 * hidden, half), f32),
            pltpu.VMEM((3, 2 * hidden, half), bf16),
            pltpu.VMEM((3, 2 * hidden, half), bf16),
            pltpu.VMEM((2 * hidden, 2 * half), bf16),
            pltpu.VMEM((2 * hidden, 2 * half), bf16),
            pltpu.VMEM((2, hidden, cols), f32),
            pltpu.VMEM((2, hidden, cols), bf16),
            pltpu.VMEM((2, hidden, cols), bf16),
            pltpu.VMEM((8, half), f32),
            pltpu.VMEM((4, 8, half), f32),
            dma((3,)),
            dma((2, 4, 4)), dma((2, 4, 4)),
            dma((3,)), dma((3,)),
            dma((3, 2 * per)), dma((3, 2 * per)),
            dma((3, 2 * per)), dma((3, 2 * per)),
            dma((2, 2 * per)), dma((2, 2 * per)),
            dma((2, per)), dma((2, per)),
            dma((4,)), dma((4,)),
        ],
        compiler_params=pltpu.CompilerParams(
            collective_id=0, has_side_effects=True, vmem_limit_bytes=60 * 1024 * 1024
        ),
    )(hot, hot_gate, tokens, cotangent, w_gate, w_up, w_down)
    count = len(ORDER) * cap
    share = lax.dynamic_slice_in_dim(share, lax.axis_index("dp") // 2 * count, count, 1)
    sums = []
    for codes in ((0, 1), (4, 5)):
        sums.append(sum(share[PLACE[c], PLACE[c] * cap : (PLACE[c] + 1) * cap] for c in codes))
    summed = jnp.concatenate(sums)
    gate_grad = jnp.sum(jnp.where(placed, summed[:, None], 0.0), axis=0)
    gate_grad = gate_grad / weight.astype(f32)
    return up, down, gate_grad.reshape(tokens.shape[0], TOP)


def partner(array, axis, bit):
    return lax.ppermute(array, axis, [(i, i ^ 1 << bit) for i in range(lax.axis_size(axis))])


def slot_of(routes, experts):
    flat = routes.reshape(-1)
    owner = (flat[:, None] == jnp.arange(experts, dtype=jnp.int32)[None, :]).astype(jnp.int32)
    before = jnp.cumsum(owner, axis=0) - owner
    slot = jnp.sum(before * owner, axis=1)
    return (flat, slot)


def shards(tokens, cotangent, routes, gates, w_gate, w_up, w_down):
    tok_count = tokens.shape[0]
    groups = lax.axis_size("expert")
    experts = groups // SPLIT
    capacity = max(2, min(TOK_DEV, 5 * TOK_DEV * TOP // (4 * experts)))
    if groups == 8 and lax.axis_size("dp") == 4 and capacity % 16 == 0 and capacity > 64 and w_gate.shape[0] % PIECE == 0:
        return fused(capacity, tokens, cotangent, routes, gates, w_gate, w_up, w_down)
    piece = (capacity + SPLIT - 1) // SPLIT
    levels = SPLIT.bit_length() - 1
    here = lax.axis_index("expert")
    flat, slot = slot_of(routes, experts)
    pair_count = flat.shape[0]
    pair_tok = (
        (jnp.arange(pair_count, dtype=jnp.int32) // TOP)[:, None]
        == jnp.arange(tok_count, dtype=jnp.int32)[None, :]
    ).astype(jnp.bfloat16)
    rows_all = groups * piece
    row_ids = jnp.arange(rows_all, dtype=jnp.int32)
    dest = row_ids // piece
    row_expert = dest // SPLIT
    row_slot = dest % SPLIT + row_ids % piece * SPLIT
    placed = (flat[None, :] == row_expert[:, None]) & (slot[None, :] == row_slot[:, None])
    placed_f = placed.astype(jnp.float32)
    token_map = jnp.dot(
        placed.astype(jnp.bfloat16), pair_tok, preferred_element_type=jnp.float32
    ).astype(jnp.bfloat16)
    send_x = jnp.dot(token_map, tokens, preferred_element_type=jnp.float32).astype(jnp.bfloat16)
    send_dy = jnp.dot(token_map, cotangent, preferred_element_type=jnp.float32).astype(jnp.bfloat16)
    send_gate = jnp.dot(
        placed_f, gates.reshape(-1).astype(jnp.float32), precision=lax.Precision.HIGHEST
    ).astype(jnp.bfloat16)
    full_gate, full_up, full_down = (
        lax.all_gather(w_gate, "dp", axis=1, tiled=True),
        lax.all_gather(w_up, "dp", axis=1, tiled=True),
        lax.all_gather(w_down, "dp", axis=1, tiled=True),
    )
    cur_x, cur_dy, cur_g = (
        lax.all_to_all(send_x, "expert", split_axis=0, concat_axis=0, tiled=True),
        lax.all_to_all(send_dy, "expert", split_axis=0, concat_axis=0, tiled=True),
        lax.all_to_all(send_gate, "expert", split_axis=0, concat_axis=0, tiled=True),
    )
    for bit in range(levels):
        got = partner((cur_x, cur_dy, cur_g), "expert", bit)
        lower = here // (1 << bit) % 2 == 0
        cur_x = jnp.where(
            lower,
            jnp.concatenate([cur_x, got[0]], axis=0),
            jnp.concatenate([got[0], cur_x], axis=0),
        )
        cur_dy = jnp.where(
            lower,
            jnp.concatenate([cur_dy, got[1]], axis=0),
            jnp.concatenate([got[1], cur_dy], axis=0),
        )
        cur_g = jnp.where(
            lower,
            jnp.concatenate([cur_g, got[2]], axis=0),
            jnp.concatenate([got[2], cur_g], axis=0),
        )
    rows_x, rows_dy, recv_gate = (cur_x, cur_dy, cur_g)
    pre_a = lax.dot_general(
        rows_x, full_gate, (((1,), (1,)), ((), ())), preferred_element_type=jnp.float32
    )
    pre_b = lax.dot_general(
        rows_x, full_up, (((1,), (1,)), ((), ())), preferred_element_type=jnp.float32
    )
    sig = jax.nn.sigmoid(pre_a)
    silu = pre_a * sig
    hidden = (silu * pre_b).astype(jnp.bfloat16)
    weight = recv_gate.astype(jnp.float32)
    probe = lax.dot_general(
        rows_dy, full_down, (((1,), (1,)), ((), ())), preferred_element_type=jnp.float32
    )
    share = jnp.sum(hidden.astype(jnp.float32) * probe, axis=1)
    scaled = (weight[:, None] * rows_dy.astype(jnp.float32)).astype(jnp.bfloat16)
    d_b = (weight[:, None] * probe * silu).astype(jnp.bfloat16)
    part_up = lax.dot_general(
        d_b, rows_x, (((0,), (0,)), ((), ())), preferred_element_type=jnp.float32
    )
    part_down = lax.dot_general(
        hidden, scaled, (((0,), (0,)), ((), ())), preferred_element_type=jnp.float32
    )
    folded = share.reshape(SPLIT, rows_all)
    for bit in reversed(range(levels)):
        half = folded.shape[0] // 2
        lower_half = folded[:half]
        upper_half = folded[half:]
        lower = here // (1 << bit) % 2 == 0
        keep = jnp.where(lower, lower_half, upper_half)
        away = jnp.where(lower, upper_half, lower_half)
        folded = keep + partner(away, "expert", bit)
    summed = lax.all_to_all(
        folded.reshape(rows_all), "expert", split_axis=0, concat_axis=0, tiled=True
    )
    gate_grad = jnp.dot(placed_f.T, summed, precision=lax.Precision.HIGHEST)
    sum_up, sum_down = (
        lax.psum_scatter(
            part_up.astype(jnp.bfloat16), "dp", scatter_dimension=1, tiled=True
        ).astype(jnp.float32),
        lax.psum_scatter(
            part_down.astype(jnp.bfloat16), "dp", scatter_dimension=1, tiled=True
        ).astype(jnp.float32),
    )
    return (
        sum_up.astype(jnp.bfloat16),
        sum_down.astype(jnp.bfloat16),
        gate_grad.reshape(tok_count, TOP),
    )


def solution(mesh):
    in_specs = (
        P(("expert", "dp"), None),
        P(("expert", "dp"), None),
        P(("expert", "dp"), None),
        P(("expert", "dp"), None),
        P("expert", "dp"),
        P("expert", "dp"),
        P("expert", "dp"),
    )
    out_specs = (P("expert", "dp"), P("expert", "dp"), P(("expert", "dp"), None))
    return jax.shard_map(shards, mesh=mesh, in_specs=in_specs, out_specs=out_specs, check_vma=False)
```

```python
import jax
import jax.numpy as jnp
from jax import lax
from jax.experimental import pallas as pl
from jax.experimental.pallas import tpu as pltpu
from jax.sharding import PartitionSpec as P

SPLIT = 4
TOP = 1
TOK_DEV = 128
MESH = pl.DeviceIdType.MESH
ORDER = (0, 1, 4, 5)
PLACE = {c: i for i, c in enumerate(ORDER)}
PIECE = 256


def flip(index, code):
    for bit in (1, 2, 4):
        if code & bit:
            index = index + bit - 2 * bit * ((index // bit) % 2)
    return index


def fused_kernel(
    cap, oh_ref, ohg_ref, tok_ref, cot_ref, wg_ref, wu_ref, wd_ref,
    up_ref, down_ref, share_ref,
    rows_x, rows_c, near, far, relay, w_all, t_sum, core_out, core_in, x_out, x_in, t_h, t_d,
    own, z_out, z_in, share_mine, share_all,
    local_sem, row_send, row_recv, far_send, far_recv, w_send, w_recv, core_send, core_recv, x_send, x_recv,
    act_send, act_recv, z_send, z_recv, share_send, share_recv,
):
    e = lax.axis_index("expert")
    d = lax.axis_index("dp")
    hidden, cols = wg_ref.shape
    half = t_sum.shape[2]
    PARTS = ((0, 256), (256, half), (0, half))
    per = hidden // PIECE
    nt = (((1,), (1,)), ((), ()))
    nn = (((1,), (0,)), ((), ()))
    f32, bf16 = jnp.float32, jnp.bfloat16
    x_here = d // 2
    x_there = 1 - x_here

    def at_device(code, rel):
        return {"expert": flip(e, code), "dp": flip(d, rel)}

    barrier = pltpu.get_barrier_semaphore()
    peers = ((0, 1), (0, 2), (0, 3), (1, 0), (2, 0), (4, 0), (5, 0))
    for code, rel in peers:
        pl.semaphore_signal(barrier, inc=1, device_id=at_device(code, rel), device_id_type=MESH)
    pl.semaphore_wait(barrier, len(peers))

    sent = []

    def plan(src, dst, send_sem, recv_sem, device):
        copy = pltpu.make_async_remote_copy(
            src_ref=src, dst_ref=dst, send_sem=send_sem, recv_sem=recv_sem,
            device_id=device, device_id_type=MESH,
        )
        sent.append(copy)
        return copy

    def push(*what):
        copy = plan(*what)
        copy.start()
        return copy

    rows = (rows_x, rows_c)
    whole = (tok_ref, cot_ref)
    hots = (oh_ref, ohg_ref)

    def block(kind, rel, source_x, code):
        number = (rel % 2) * 8 + PLACE[code] * 2 + source_x
        return rows[kind].at[pl.ds(pl.multiple_of(number * cap, 16), cap), :]

    def pick(kind, low, rel):
        lanes = pl.ds(pl.multiple_of(flip(d, rel) * cols, 128), cols)
        return lax.dot_general(
            hots[kind][low : low + cap, :], whole[kind][:, lanes], nn, preferred_element_type=f32
        ).astype(bf16)

    row_copy = {}

    def send_block(kind, code, rel, source, there, source_x, device):
        row_copy[kind, code, rel] = push(
            source, there, row_send.at[kind, PLACE[code], rel], row_recv.at[kind, PLACE[code], rel], device
        )

    far_copy = {}

    def send_far(kind, rel):
        far[kind, rel] = pick(kind, cap, rel)
        if rel:
            far_copy[kind, rel] = push(
                far.at[kind, rel], relay.at[kind, rel - 1],
                far_send.at[kind, rel], far_recv.at[kind, rel], at_device(0, rel),
            )

    def go_far(kind, rel):
        if rel:
            far_copy[kind, rel].wait_recv()
        source = relay.at[kind, rel - 1] if rel else far.at[kind, 0]
        source_x = x_there if rel // 2 else x_here
        send_block(kind, 4, rel, source, block(kind, rel, source_x, 4), source_x, at_device(4, 0))

    def send_near(kind, rel):
        if rel == 0:
            mine = block(kind, 0, x_here, 0)
            mine[...] = pick(kind, 0, 0)
        else:
            near[kind, rel - 1] = pick(kind, 0, rel)
            send_block(
                kind, 0, rel, near.at[kind, rel - 1], block(kind, rel, x_here, 0), x_here, at_device(0, rel)
            )

    def pass_on(kind, code, rel):
        source_x = x_there if rel // 2 else x_here
        send_block(
            kind, code + 1, rel, block(kind, rel, source_x, code), block(kind, rel, source_x, code + 1),
            source_x, at_device(1, 0),
        )

    def got(kind, code, rel):
        row_copy[kind, code, rel].wait_recv()

    def forward(kind, code, rel):
        got(kind, code, rel)
        pass_on(kind, code, rel)

    w_in = (wg_ref, wu_ref, wd_ref)
    w_copy = {}
    local = {}

    for k in (0, 1, 2):
        w_copy[k] = plan(
            w_in[k], w_all.at[k, hidden : 2 * hidden], w_send.at[k], w_recv.at[k], at_device(2, 0)
        )

    def w_own(k, core):
        @pl.when(d % 2 == core)
        def _():
            w_copy[k].start()

    def w_keep(k):
        local[k] = pltpu.make_async_copy(w_in[k], w_all.at[k, 0:hidden], local_sem.at[k])
        local[k].start()

    def span(q):
        return slice(q * PIECE, (q + 1) * PIECE)

    core_copy = {}
    x_copy = {}
    act_copy = {}
    z_copy = {}

    def project(k, q, part):
        low, high = PARTS[part]
        weight = w_all[k, span(q), :]
        core_out[k, span(q), low:high] = lax.dot_general(
            weight, rows[k // 2][half + low : half + high, :], nt, preferred_element_type=f32
        )
        core_copy[k, q, part] = push(
            core_out.at[k, span(q), low:high], core_in.at[k, span(q), low:high],
            core_send.at[k, q, part], core_recv.at[k, q, part], at_device(0, 1),
        )
        t_sum[k, span(q), low:high] = lax.dot_general(
            weight, rows[k // 2][low:high, :], nt, preferred_element_type=f32
        )

    def cross(k, q, part):
        low, high = PARTS[part]
        core_copy[k, q, part].wait_recv()
        both = t_sum[k, span(q), low:high] + core_in[k, span(q), low:high]
        x_out[k, span(q), low:high] = both.astype(bf16)
        x_copy[k, q, part] = push(
            x_out.at[k, span(q), low:high], x_in.at[k, span(q), low:high],
            x_send.at[k, q, part], x_recv.at[k, q, part], at_device(0, 2),
        )
        t_sum[k, span(q), low:high] = both

    def total(k, q):
        for part in (0, 1, 2):
            if (k, q, part) in x_copy:
                x_copy[k, q, part].wait_recv()
        return t_sum[k, span(q), :] + x_in[k, span(q), :].astype(f32)

    def hand_over(g, ref, q):
        act_copy[g, q] = push(
            ref.at[span(q), 0:half], ref.at[span(q), half : 2 * half],
            act_send.at[g, q], act_recv.at[g, q], at_device(0, 1),
        )

    def activate(q):
        a = total(0, q)
        silu = a * jax.nn.sigmoid(a)
        t_h[span(q), 0:half] = (silu * total(1, q)).astype(bf16)
        hand_over(1, t_h, q)
        t_sum[0, span(q), :] = silu

    def derive(q):
        p = total(2, q)
        t_d[span(q), 0:half] = (p * t_sum[0, span(q), :]).astype(bf16)
        hand_over(0, t_d, q)
        t_sum[2, span(q), :] = p

    left = (t_d, t_h)

    def gradient(g, q):
        act_copy[g, q].wait_recv()
        out = lax.dot_general(
            left[g][span(q), :], rows[g][...], nn, preferred_element_type=f32
        )
        if q < per:
            own[g, span(q), :] = out
        else:
            there = span(q - per)
            z_out[g, there, :] = out.astype(bf16)
            z_copy[g, q - per] = push(
                z_out.at[g, there], z_in.at[g, there],
                z_send.at[g, q - per], z_recv.at[g, q - per], at_device(2, 0),
            )

    mine_q = tuple(range(per))
    their_q = tuple(range(per, 2 * per))

    def do_project(k, qs, part):
        for q in qs:
            project(k, q, part)

    def do_cross(k, qs, part):
        for q in qs:
            cross(k, q, part)

    def all_got(kind, code):
        for rel in (0, 1, 2, 3):
            got(kind, code, rel)

    for rel in (2, 3, 1, 0):
        send_far(0, rel)
    w_own(0, 1)
    go_far(0, 0)
    send_near(0, 0)
    pass_on(0, 0, 0)
    for rel in (2, 3, 1):
        send_near(0, rel)
    go_far(0, 1)
    for rel in (2, 3, 1, 0):
        send_far(1, rel)
    forward(0, 0, 1)
    for rel in (2, 3, 1, 0):
        send_near(1, rel)
    for k in (0, 1, 2):
        w_keep(k)
    go_far(0, 2)
    go_far(0, 3)
    w_own(0, 0)
    w_own(1, 1)
    go_far(1, 0)
    go_far(1, 1)
    forward(0, 4, 0)
    forward(0, 0, 2)
    forward(0, 0, 3)
    forward(0, 4, 1)
    pass_on(1, 0, 0)
    go_far(1, 2)
    go_far(1, 3)
    w_own(1, 0)
    w_own(2, 0)
    w_own(2, 1)
    all_got(0, 1)
    local[0].wait()
    do_project(0, mine_q, 0)
    local[1].wait()
    do_project(1, mine_q, 0)
    do_cross(0, mine_q, 0)
    do_cross(1, mine_q, 0)
    forward(0, 4, 2)
    forward(1, 0, 1)
    w_copy[0].wait_recv()
    do_project(0, their_q, 0)
    do_cross(0, their_q, 0)
    forward(0, 4, 3)
    forward(1, 0, 2)
    forward(1, 0, 3)
    all_got(0, 5)
    do_project(0, mine_q, 1)
    do_project(1, mine_q, 1)
    do_cross(0, mine_q, 1)
    do_cross(1, mine_q, 1)
    forward(1, 4, 0)
    do_project(0, their_q, 1)
    do_cross(0, their_q, 1)
    forward(1, 4, 1)
    w_copy[1].wait_recv()
    do_project(1, their_q, 2)
    do_cross(1, their_q, 2)
    forward(1, 4, 2)
    for q in mine_q:
        activate(q)
    forward(1, 4, 3)
    all_got(1, 1)
    all_got(1, 5)
    w_copy[2].wait_recv()
    do_project(2, their_q, 2)
    do_cross(2, their_q, 2)
    local[2].wait()
    do_project(2, mine_q, 2)
    do_cross(2, mine_q, 2)
    for q in their_q:
        activate(q)
    for q in their_q:
        gradient(1, q)
    for q in mine_q:
        gradient(1, q)
    for q in their_q:
        derive(q)
        gradient(0, q)
    for q in mine_q:
        derive(q)
    dots = jnp.sum(t_h[:, 0:half].astype(f32) * t_sum[2], axis=0, keepdims=True)
    share_mine[...] = jnp.broadcast_to(dots, share_mine.shape)
    share_copy = {}
    for code in (1, 4, 5):
        n = PLACE[code]
        share_copy[n] = push(
            share_mine, share_all.at[n], share_send.at[n], share_recv.at[n], at_device(code, 0)
        )
    share_ref[0:1, :] = share_mine[0:1, :]
    for q in mine_q:
        gradient(0, q)
    for g, out in ((1, down_ref), (0, up_ref)):
        for q in mine_q:
            z_copy[g, q].wait_recv()
            out[span(q), :] = (own[g, span(q), :] + z_in[g, span(q), :].astype(f32)).astype(bf16)
    for n in (1, 2, 3):
        share_copy[n].wait_recv()
        share_ref[n : n + 1, :] = share_all[n, 0:1, :]
    for copy in sent:
        copy.wait_send()


def fused(cap, tokens, cotangent, routes, gates, w_gate, w_up, w_down):
    near = lax.axis_index("expert") // SPLIT
    flat, slot = slot_of(routes, 2)
    ids = jnp.arange(2 * cap, dtype=jnp.int32)
    named = jnp.where(ids < cap, near, 1 - near)
    placed = (flat[None, :] == named[:, None]) & (slot[None, :] == (ids % cap)[:, None])
    hot = placed.astype(jnp.bfloat16)
    weight = gates.reshape(-1)
    hot_gate = jnp.where(placed, weight[None, :], jnp.zeros((), jnp.bfloat16))
    hidden, cols = w_gate.shape
    half = 8 * cap
    per = hidden // PIECE
    bf16, f32 = jnp.bfloat16, jnp.float32
    vmem = pl.BlockSpec(memory_space=pltpu.VMEM)
    anywhere = pl.BlockSpec(memory_space=pl.ANY)
    dma = pltpu.SemaphoreType.DMA
    up, down, share = pl.pallas_call(
        lambda *refs: fused_kernel(cap, *refs),
        out_shape=(
            jax.ShapeDtypeStruct((hidden, cols), bf16),
            jax.ShapeDtypeStruct((hidden, cols), bf16),
            jax.ShapeDtypeStruct((4, half), f32),
        ),
        in_specs=[vmem] * 4 + [anywhere] * 3,
        out_specs=(vmem, vmem, vmem),
        scratch_shapes=[
            pltpu.VMEM((2 * half, cols), bf16),
            pltpu.VMEM((2 * half, cols), bf16),
            pltpu.VMEM((2, 3, cap, cols), bf16),
            pltpu.VMEM((2, 4, cap, cols), bf16),
            pltpu.VMEM((2, 3, cap, cols), bf16),
            pltpu.VMEM((3, 2 * hidden, cols), bf16),
            pltpu.VMEM((3, 2 * hidden, half), f32),
            pltpu.VMEM((3, 2 * hidden, half), f32),
            pltpu.VMEM((3, 2 * hidden, half), f32),
            pltpu.VMEM((3, 2 * hidden, half), bf16),
            pltpu.VMEM((3, 2 * hidden, half), bf16),
            pltpu.VMEM((2 * hidden, 2 * half), bf16),
            pltpu.VMEM((2 * hidden, 2 * half), bf16),
            pltpu.VMEM((2, hidden, cols), f32),
            pltpu.VMEM((2, hidden, cols), bf16),
            pltpu.VMEM((2, hidden, cols), bf16),
            pltpu.VMEM((8, half), f32),
            pltpu.VMEM((4, 8, half), f32),
            dma((3,)),
            dma((2, 4, 4)), dma((2, 4, 4)),
            dma((2, 4)), dma((2, 4)),
            dma((3,)), dma((3,)),
            dma((3, 2 * per, 3)), dma((3, 2 * per, 3)),
            dma((3, 2 * per, 3)), dma((3, 2 * per, 3)),
            dma((2, 2 * per)), dma((2, 2 * per)),
            dma((2, per)), dma((2, per)),
            dma((4,)), dma((4,)),
        ],
        compiler_params=pltpu.CompilerParams(
            collective_id=0, has_side_effects=True, vmem_limit_bytes=60 * 1024 * 1024
        ),
    )(hot, hot_gate, tokens, cotangent, w_gate, w_up, w_down)
    share = share.reshape(4, 4, 2, cap)
    share = lax.dynamic_index_in_dim(share, lax.axis_index("dp") // 2, 2, False)
    sums = []
    for codes in ((0, 1), (4, 5)):
        sums.append(sum(share[PLACE[c], PLACE[c]] for c in codes))
    summed = jnp.concatenate(sums)
    gate_grad = jnp.sum(jnp.where(placed, summed[:, None], 0.0), axis=0)
    gate_grad = gate_grad / weight.astype(f32)
    return up, down, gate_grad.reshape(tokens.shape[0], TOP)


def partner(array, axis, bit):
    return lax.ppermute(array, axis, [(i, i ^ 1 << bit) for i in range(lax.axis_size(axis))])


def slot_of(routes, experts):
    flat = routes.reshape(-1)
    owner = (flat[:, None] == jnp.arange(experts, dtype=jnp.int32)[None, :]).astype(jnp.int32)
    before = jnp.cumsum(owner, axis=0) - owner
    slot = jnp.sum(before * owner, axis=1)
    return (flat, slot)


def shards(tokens, cotangent, routes, gates, w_gate, w_up, w_down):
    tok_count = tokens.shape[0]
    groups = lax.axis_size("expert")
    experts = groups // SPLIT
    capacity = max(2, min(TOK_DEV, 5 * TOK_DEV * TOP // (4 * experts)))
    if groups == 8 and lax.axis_size("dp") == 4 and capacity % 16 == 0 and capacity > 64 and w_gate.shape[0] % PIECE == 0:
        return fused(capacity, tokens, cotangent, routes, gates, w_gate, w_up, w_down)
    piece = (capacity + SPLIT - 1) // SPLIT
    levels = SPLIT.bit_length() - 1
    here = lax.axis_index("expert")
    flat, slot = slot_of(routes, experts)
    pair_count = flat.shape[0]
    pair_tok = (
        (jnp.arange(pair_count, dtype=jnp.int32) // TOP)[:, None]
        == jnp.arange(tok_count, dtype=jnp.int32)[None, :]
    ).astype(jnp.bfloat16)
    rows_all = groups * piece
    row_ids = jnp.arange(rows_all, dtype=jnp.int32)
    dest = row_ids // piece
    row_expert = dest // SPLIT
    row_slot = dest % SPLIT + row_ids % piece * SPLIT
    placed = (flat[None, :] == row_expert[:, None]) & (slot[None, :] == row_slot[:, None])
    placed_f = placed.astype(jnp.float32)
    token_map = jnp.dot(
        placed.astype(jnp.bfloat16), pair_tok, preferred_element_type=jnp.float32
    ).astype(jnp.bfloat16)
    send_x = jnp.dot(token_map, tokens, preferred_element_type=jnp.float32).astype(jnp.bfloat16)
    send_dy = jnp.dot(token_map, cotangent, preferred_element_type=jnp.float32).astype(jnp.bfloat16)
    send_gate = jnp.dot(
        placed_f, gates.reshape(-1).astype(jnp.float32), precision=lax.Precision.HIGHEST
    ).astype(jnp.bfloat16)
    full_gate, full_up, full_down = (
        lax.all_gather(w_gate, "dp", axis=1, tiled=True),
        lax.all_gather(w_up, "dp", axis=1, tiled=True),
        lax.all_gather(w_down, "dp", axis=1, tiled=True),
    )
    cur_x, cur_dy, cur_g = (
        lax.all_to_all(send_x, "expert", split_axis=0, concat_axis=0, tiled=True),
        lax.all_to_all(send_dy, "expert", split_axis=0, concat_axis=0, tiled=True),
        lax.all_to_all(send_gate, "expert", split_axis=0, concat_axis=0, tiled=True),
    )
    for bit in range(levels):
        got = partner((cur_x, cur_dy, cur_g), "expert", bit)
        lower = here // (1 << bit) % 2 == 0
        cur_x = jnp.where(
            lower,
            jnp.concatenate([cur_x, got[0]], axis=0),
            jnp.concatenate([got[0], cur_x], axis=0),
        )
        cur_dy = jnp.where(
            lower,
            jnp.concatenate([cur_dy, got[1]], axis=0),
            jnp.concatenate([got[1], cur_dy], axis=0),
        )
        cur_g = jnp.where(
            lower,
            jnp.concatenate([cur_g, got[2]], axis=0),
            jnp.concatenate([got[2], cur_g], axis=0),
        )
    rows_x, rows_dy, recv_gate = (cur_x, cur_dy, cur_g)
    pre_a = lax.dot_general(
        rows_x, full_gate, (((1,), (1,)), ((), ())), preferred_element_type=jnp.float32
    )
    pre_b = lax.dot_general(
        rows_x, full_up, (((1,), (1,)), ((), ())), preferred_element_type=jnp.float32
    )
    sig = jax.nn.sigmoid(pre_a)
    silu = pre_a * sig
    hidden = (silu * pre_b).astype(jnp.bfloat16)
    weight = recv_gate.astype(jnp.float32)
    probe = lax.dot_general(
        rows_dy, full_down, (((1,), (1,)), ((), ())), preferred_element_type=jnp.float32
    )
    share = jnp.sum(hidden.astype(jnp.float32) * probe, axis=1)
    scaled = (weight[:, None] * rows_dy.astype(jnp.float32)).astype(jnp.bfloat16)
    d_b = (weight[:, None] * probe * silu).astype(jnp.bfloat16)
    part_up = lax.dot_general(
        d_b, rows_x, (((0,), (0,)), ((), ())), preferred_element_type=jnp.float32
    )
    part_down = lax.dot_general(
        hidden, scaled, (((0,), (0,)), ((), ())), preferred_element_type=jnp.float32
    )
    folded = share.reshape(SPLIT, rows_all)
    for bit in reversed(range(levels)):
        half = folded.shape[0] // 2
        lower_half = folded[:half]
        upper_half = folded[half:]
        lower = here // (1 << bit) % 2 == 0
        keep = jnp.where(lower, lower_half, upper_half)
        away = jnp.where(lower, upper_half, lower_half)
        folded = keep + partner(away, "expert", bit)
    summed = lax.all_to_all(
        folded.reshape(rows_all), "expert", split_axis=0, concat_axis=0, tiled=True
    )
    gate_grad = jnp.dot(placed_f.T, summed, precision=lax.Precision.HIGHEST)
    sum_up, sum_down = (
        lax.psum_scatter(
            part_up.astype(jnp.bfloat16), "dp", scatter_dimension=1, tiled=True
        ).astype(jnp.float32),
        lax.psum_scatter(
            part_down.astype(jnp.bfloat16), "dp", scatter_dimension=1, tiled=True
        ).astype(jnp.float32),
    )
    return (
        sum_up.astype(jnp.bfloat16),
        sum_down.astype(jnp.bfloat16),
        gate_grad.reshape(tok_count, TOP),
    )


def solution(mesh):
    in_specs = (
        P(("expert", "dp"), None),
        P(("expert", "dp"), None),
        P(("expert", "dp"), None),
        P(("expert", "dp"), None),
        P("expert", "dp"),
        P("expert", "dp"),
        P("expert", "dp"),
    )
    out_specs = (P("expert", "dp"), P("expert", "dp"), P(("expert", "dp"), None))
    return jax.shard_map(shards, mesh=mesh, in_specs=in_specs, out_specs=out_specs, check_vma=False)
```

```python
import jax
import jax.numpy as jnp
from jax import lax
from jax.experimental import pallas as pl
from jax.experimental.pallas import tpu as pltpu
from jax.sharding import PartitionSpec as P

SPLIT = 4
TOP = 1
TOK_DEV = 128
MESH = pl.DeviceIdType.MESH
ORDER = (0, 1, 4, 5)
PLACE = {c: i for i, c in enumerate(ORDER)}
PIECE = 256


def flip(index, code):
    for bit in (1, 2, 4):
        if code & bit:
            index = index + bit - 2 * bit * ((index // bit) % 2)
    return index


def fused_kernel(
    cap, oh_ref, ohg_ref, tok_ref, cot_ref, wg_ref, wu_ref, wd_ref,
    up_ref, down_ref, share_ref,
    rows_x, rows_c, near, far, relay, w_all, t_sum, core_out, core_in, x_out, x_in, t_h, t_d,
    own, z_out, z_in, share_mine, share_all,
    local_sem, row_send, row_recv, far_send, far_recv, w_send, w_recv, core_send, core_recv, x_send, x_recv,
    act_send, act_recv, z_send, z_recv, share_send, share_recv,
):
    e = lax.axis_index("expert")
    d = lax.axis_index("dp")
    hidden, cols = wg_ref.shape
    half = t_sum.shape[2]
    PARTS = ((0, 256), (256, half), (0, half))
    per = hidden // PIECE
    nt = (((1,), (1,)), ((), ()))
    nn = (((1,), (0,)), ((), ()))
    f32, bf16 = jnp.float32, jnp.bfloat16
    x_here = d // 2
    x_there = 1 - x_here

    def at_device(code, rel):
        return {"expert": flip(e, code), "dp": flip(d, rel)}

    barrier = pltpu.get_barrier_semaphore()
    peers = ((0, 1), (0, 2), (0, 3), (1, 0), (2, 0), (4, 0), (5, 0))
    for code, rel in peers:
        pl.semaphore_signal(barrier, inc=1, device_id=at_device(code, rel), device_id_type=MESH)
    pl.semaphore_wait(barrier, len(peers))

    sent = []

    def plan(src, dst, send_sem, recv_sem, device):
        copy = pltpu.make_async_remote_copy(
            src_ref=src, dst_ref=dst, send_sem=send_sem, recv_sem=recv_sem,
            device_id=device, device_id_type=MESH,
        )
        sent.append(copy)
        return copy

    def push(*what):
        copy = plan(*what)
        copy.start()
        return copy

    rows = (rows_x, rows_c)
    whole = (tok_ref, cot_ref)
    hots = (oh_ref, ohg_ref)

    def block(kind, rel, source_x, code):
        number = (rel % 2) * 8 + PLACE[code] * 2 + source_x
        return rows[kind].at[pl.ds(pl.multiple_of(number * cap, 16), cap), :]

    def pick(kind, low, rel):
        lanes = pl.ds(pl.multiple_of(flip(d, rel) * cols, 128), cols)
        return lax.dot_general(
            hots[kind][low : low + cap, :], whole[kind][:, lanes], nn, preferred_element_type=f32
        ).astype(bf16)

    row_copy = {}

    def send_block(kind, code, rel, source, there, source_x, device):
        row_copy[kind, code, rel] = push(
            source, there, row_send.at[kind, PLACE[code], rel], row_recv.at[kind, PLACE[code], rel], device
        )

    far_copy = {}

    def send_far(kind, rel):
        far[kind, rel] = pick(kind, cap, rel)
        if rel:
            far_copy[kind, rel] = push(
                far.at[kind, rel], relay.at[kind, rel - 1],
                far_send.at[kind, rel], far_recv.at[kind, rel], at_device(0, rel),
            )

    def go_far(kind, rel):
        if rel:
            far_copy[kind, rel].wait_recv()
        source = relay.at[kind, rel - 1] if rel else far.at[kind, 0]
        source_x = x_there if rel // 2 else x_here
        send_block(kind, 4, rel, source, block(kind, rel, source_x, 4), source_x, at_device(4, 0))

    def send_near(kind, rel):
        if rel == 0:
            mine = block(kind, 0, x_here, 0)
            mine[...] = pick(kind, 0, 0)
        else:
            near[kind, rel - 1] = pick(kind, 0, rel)
            send_block(
                kind, 0, rel, near.at[kind, rel - 1], block(kind, rel, x_here, 0), x_here, at_device(0, rel)
            )

    def pass_on(kind, code, rel):
        source_x = x_there if rel // 2 else x_here
        send_block(
            kind, code + 1, rel, block(kind, rel, source_x, code), block(kind, rel, source_x, code + 1),
            source_x, at_device(1, 0),
        )

    def got(kind, code, rel):
        row_copy[kind, code, rel].wait_recv()

    def forward(kind, code, rel):
        got(kind, code, rel)
        pass_on(kind, code, rel)

    w_in = (wg_ref, wu_ref, wd_ref)
    w_copy = {}
    local = {}

    for k in (0, 1, 2):
        w_copy[k] = plan(
            w_in[k], w_all.at[k, hidden : 2 * hidden], w_send.at[k], w_recv.at[k], at_device(2, 0)
        )

    def w_own(k, core):
        @pl.when(d % 2 == core)
        def _():
            w_copy[k].start()

    def w_keep(k):
        local[k] = pltpu.make_async_copy(w_in[k], w_all.at[k, 0:hidden], local_sem.at[k])
        local[k].start()

    def span(q):
        return slice(q * PIECE, (q + 1) * PIECE)

    core_copy = {}
    x_copy = {}
    act_copy = {}
    z_copy = {}

    def project(k, q, part):
        low, high = PARTS[part]
        weight = w_all[k, span(q), :]
        core_out[k, span(q), low:high] = lax.dot_general(
            weight, rows[k // 2][half + low : half + high, :], nt, preferred_element_type=f32
        )
        core_copy[k, q, part] = push(
            core_out.at[k, span(q), low:high], core_in.at[k, span(q), low:high],
            core_send.at[k, q, part], core_recv.at[k, q, part], at_device(0, 1),
        )
        t_sum[k, span(q), low:high] = lax.dot_general(
            weight, rows[k // 2][low:high, :], nt, preferred_element_type=f32
        )

    def cross(k, q, part):
        low, high = PARTS[part]
        core_copy[k, q, part].wait_recv()
        both = t_sum[k, span(q), low:high] + core_in[k, span(q), low:high]
        x_out[k, span(q), low:high] = both.astype(bf16)
        x_copy[k, q, part] = push(
            x_out.at[k, span(q), low:high], x_in.at[k, span(q), low:high],
            x_send.at[k, q, part], x_recv.at[k, q, part], at_device(0, 2),
        )
        t_sum[k, span(q), low:high] = both

    def total(k, q):
        for part in (0, 1, 2):
            if (k, q, part) in x_copy:
                x_copy[k, q, part].wait_recv()
        return t_sum[k, span(q), :] + x_in[k, span(q), :].astype(f32)

    def hand_over(g, ref, q):
        act_copy[g, q] = push(
            ref.at[span(q), 0:half], ref.at[span(q), half : 2 * half],
            act_send.at[g, q], act_recv.at[g, q], at_device(0, 1),
        )

    def activate(q):
        a = total(0, q)
        silu = a * jax.nn.sigmoid(a)
        t_h[span(q), 0:half] = (silu * total(1, q)).astype(bf16)
        hand_over(1, t_h, q)
        t_sum[0, span(q), :] = silu

    def derive(q):
        p = total(2, q)
        t_d[span(q), 0:half] = (p * t_sum[0, span(q), :]).astype(bf16)
        hand_over(0, t_d, q)
        t_sum[2, span(q), :] = p

    left = (t_d, t_h)

    def gradient(g, q):
        act_copy[g, q].wait_recv()
        out = lax.dot_general(
            left[g][span(q), :], rows[g][...], nn, preferred_element_type=f32
        )
        if q < per:
            own[g, span(q), :] = out
        else:
            there = span(q - per)
            z_out[g, there, :] = out.astype(bf16)
            z_copy[g, q - per] = push(
                z_out.at[g, there], z_in.at[g, there],
                z_send.at[g, q - per], z_recv.at[g, q - per], at_device(2, 0),
            )

    mine_q = tuple(range(per))
    their_q = tuple(range(per, 2 * per))

    def do_project(k, qs, part):
        for q in qs:
            project(k, q, part)

    def do_cross(k, qs, part):
        for q in qs:
            cross(k, q, part)

    def all_got(kind, code):
        for rel in (0, 1, 2, 3):
            got(kind, code, rel)

    for rel in (2, 3, 1, 0):
        send_far(0, rel)
    w_own(0, 1)
    go_far(0, 0)
    send_near(0, 0)
    pass_on(0, 0, 0)
    for rel in (2, 3, 1):
        send_near(0, rel)
    go_far(0, 1)
    for rel in (2, 3, 1, 0):
        send_far(1, rel)
    forward(0, 0, 1)
    for rel in (2, 3, 1, 0):
        send_near(1, rel)
    pass_on(1, 0, 0)
    for k in (0, 1, 2):
        w_keep(k)
    go_far(0, 2)
    go_far(0, 3)
    w_own(0, 0)
    w_own(1, 1)
    go_far(1, 0)
    go_far(1, 1)
    forward(0, 4, 0)
    forward(0, 0, 2)
    forward(0, 0, 3)
    forward(0, 4, 1)
    go_far(1, 2)
    go_far(1, 3)
    w_own(1, 0)
    w_own(2, 0)
    w_own(2, 1)
    all_got(0, 1)
    local[0].wait()
    do_project(0, mine_q, 0)
    local[1].wait()
    do_project(1, mine_q, 0)
    do_cross(0, mine_q, 0)
    do_cross(1, mine_q, 0)
    forward(0, 4, 2)
    forward(1, 0, 1)
    w_copy[0].wait_recv()
    do_project(0, their_q, 0)
    do_cross(0, their_q, 0)
    forward(0, 4, 3)
    forward(1, 0, 2)
    forward(1, 0, 3)
    all_got(0, 5)
    do_project(0, mine_q, 1)
    do_cross(0, mine_q, 1)
    do_project(0, their_q, 1)
    do_cross(0, their_q, 1)
    forward(1, 4, 0)
    do_project(1, mine_q, 1)
    forward(1, 4, 1)
    w_copy[1].wait_recv()
    do_project(1, their_q, 2)
    do_cross(1, their_q, 2)
    do_cross(1, mine_q, 1)
    forward(1, 4, 2)
    forward(1, 4, 3)
    all_got(1, 1)
    w_copy[2].wait_recv()
    all_got(1, 5)
    do_project(2, their_q, 2)
    do_cross(2, their_q, 2)
    for q in their_q:
        activate(q)
    local[2].wait()
    do_project(2, mine_q, 2)
    for q in their_q:
        gradient(1, q)
    do_cross(2, mine_q, 2)
    for q in mine_q:
        activate(q)
    for q in mine_q:
        gradient(1, q)
    for q in their_q:
        derive(q)
        gradient(0, q)
    for q in mine_q:
        derive(q)
    dots = jnp.sum(t_h[:, 0:half].astype(f32) * t_sum[2], axis=0, keepdims=True)
    share_mine[...] = jnp.broadcast_to(dots, share_mine.shape)
    share_copy = {}
    for code in (1, 4, 5):
        n = PLACE[code]
        share_copy[n] = push(
            share_mine, share_all.at[n], share_send.at[n], share_recv.at[n], at_device(code, 0)
        )
    share_ref[0:1, :] = share_mine[0:1, :]
    for q in mine_q:
        gradient(0, q)
    for g, out in ((1, down_ref), (0, up_ref)):
        for q in mine_q:
            z_copy[g, q].wait_recv()
            out[span(q), :] = (own[g, span(q), :] + z_in[g, span(q), :].astype(f32)).astype(bf16)
    for n in (1, 2, 3):
        share_copy[n].wait_recv()
        share_ref[n : n + 1, :] = share_all[n, 0:1, :]
    for copy in sent:
        copy.wait_send()


def fused(cap, tokens, cotangent, routes, gates, w_gate, w_up, w_down):
    near = lax.axis_index("expert") // SPLIT
    flat, slot = slot_of(routes, 2)
    ids = jnp.arange(2 * cap, dtype=jnp.int32)
    named = jnp.where(ids < cap, near, 1 - near)
    placed = (flat[None, :] == named[:, None]) & (slot[None, :] == (ids % cap)[:, None])
    hot = placed.astype(jnp.bfloat16)
    weight = gates.reshape(-1)
    hot_gate = jnp.where(placed, weight[None, :], jnp.zeros((), jnp.bfloat16))
    hidden, cols = w_gate.shape
    half = 8 * cap
    per = hidden // PIECE
    bf16, f32 = jnp.bfloat16, jnp.float32
    vmem = pl.BlockSpec(memory_space=pltpu.VMEM)
    anywhere = pl.BlockSpec(memory_space=pl.ANY)
    dma = pltpu.SemaphoreType.DMA
    up, down, share = pl.pallas_call(
        lambda *refs: fused_kernel(cap, *refs),
        out_shape=(
            jax.ShapeDtypeStruct((hidden, cols), bf16),
            jax.ShapeDtypeStruct((hidden, cols), bf16),
            jax.ShapeDtypeStruct((4, half), f32),
        ),
        in_specs=[vmem] * 4 + [anywhere] * 3,
        out_specs=(vmem, vmem, vmem),
        scratch_shapes=[
            pltpu.VMEM((2 * half, cols), bf16),
            pltpu.VMEM((2 * half, cols), bf16),
            pltpu.VMEM((2, 3, cap, cols), bf16),
            pltpu.VMEM((2, 4, cap, cols), bf16),
            pltpu.VMEM((2, 3, cap, cols), bf16),
            pltpu.VMEM((3, 2 * hidden, cols), bf16),
            pltpu.VMEM((3, 2 * hidden, half), f32),
            pltpu.VMEM((3, 2 * hidden, half), f32),
            pltpu.VMEM((3, 2 * hidden, half), f32),
            pltpu.VMEM((3, 2 * hidden, half), bf16),
            pltpu.VMEM((3, 2 * hidden, half), bf16),
            pltpu.VMEM((2 * hidden, 2 * half), bf16),
            pltpu.VMEM((2 * hidden, 2 * half), bf16),
            pltpu.VMEM((2, hidden, cols), f32),
            pltpu.VMEM((2, hidden, cols), bf16),
            pltpu.VMEM((2, hidden, cols), bf16),
            pltpu.VMEM((8, half), f32),
            pltpu.VMEM((4, 8, half), f32),
            dma((3,)),
            dma((2, 4, 4)), dma((2, 4, 4)),
            dma((2, 4)), dma((2, 4)),
            dma((3,)), dma((3,)),
            dma((3, 2 * per, 3)), dma((3, 2 * per, 3)),
            dma((3, 2 * per, 3)), dma((3, 2 * per, 3)),
            dma((2, 2 * per)), dma((2, 2 * per)),
            dma((2, per)), dma((2, per)),
            dma((4,)), dma((4,)),
        ],
        compiler_params=pltpu.CompilerParams(
            collective_id=0, has_side_effects=True, vmem_limit_bytes=60 * 1024 * 1024
        ),
    )(hot, hot_gate, tokens, cotangent, w_gate, w_up, w_down)
    share = share.reshape(4, 4, 2, cap)
    share = lax.dynamic_index_in_dim(share, lax.axis_index("dp") // 2, 2, False)
    sums = []
    for codes in ((0, 1), (4, 5)):
        sums.append(sum(share[PLACE[c], PLACE[c]] for c in codes))
    summed = jnp.concatenate(sums)
    gate_grad = jnp.sum(jnp.where(placed, summed[:, None], 0.0), axis=0)
    gate_grad = gate_grad / weight.astype(f32)
    return up, down, gate_grad.reshape(tokens.shape[0], TOP)


def partner(array, axis, bit):
    return lax.ppermute(array, axis, [(i, i ^ 1 << bit) for i in range(lax.axis_size(axis))])


def slot_of(routes, experts):
    flat = routes.reshape(-1)
    owner = (flat[:, None] == jnp.arange(experts, dtype=jnp.int32)[None, :]).astype(jnp.int32)
    before = jnp.cumsum(owner, axis=0) - owner
    slot = jnp.sum(before * owner, axis=1)
    return (flat, slot)


def shards(tokens, cotangent, routes, gates, w_gate, w_up, w_down):
    tok_count = tokens.shape[0]
    groups = lax.axis_size("expert")
    experts = groups // SPLIT
    capacity = max(2, min(TOK_DEV, 5 * TOK_DEV * TOP // (4 * experts)))
    if groups == 8 and lax.axis_size("dp") == 4 and capacity % 16 == 0 and capacity > 64 and w_gate.shape[0] % PIECE == 0:
        return fused(capacity, tokens, cotangent, routes, gates, w_gate, w_up, w_down)
    piece = (capacity + SPLIT - 1) // SPLIT
    levels = SPLIT.bit_length() - 1
    here = lax.axis_index("expert")
    flat, slot = slot_of(routes, experts)
    pair_count = flat.shape[0]
    pair_tok = (
        (jnp.arange(pair_count, dtype=jnp.int32) // TOP)[:, None]
        == jnp.arange(tok_count, dtype=jnp.int32)[None, :]
    ).astype(jnp.bfloat16)
    rows_all = groups * piece
    row_ids = jnp.arange(rows_all, dtype=jnp.int32)
    dest = row_ids // piece
    row_expert = dest // SPLIT
    row_slot = dest % SPLIT + row_ids % piece * SPLIT
    placed = (flat[None, :] == row_expert[:, None]) & (slot[None, :] == row_slot[:, None])
    placed_f = placed.astype(jnp.float32)
    token_map = jnp.dot(
        placed.astype(jnp.bfloat16), pair_tok, preferred_element_type=jnp.float32
    ).astype(jnp.bfloat16)
    send_x = jnp.dot(token_map, tokens, preferred_element_type=jnp.float32).astype(jnp.bfloat16)
    send_dy = jnp.dot(token_map, cotangent, preferred_element_type=jnp.float32).astype(jnp.bfloat16)
    send_gate = jnp.dot(
        placed_f, gates.reshape(-1).astype(jnp.float32), precision=lax.Precision.HIGHEST
    ).astype(jnp.bfloat16)
    full_gate, full_up, full_down = (
        lax.all_gather(w_gate, "dp", axis=1, tiled=True),
        lax.all_gather(w_up, "dp", axis=1, tiled=True),
        lax.all_gather(w_down, "dp", axis=1, tiled=True),
    )
    cur_x, cur_dy, cur_g = (
        lax.all_to_all(send_x, "expert", split_axis=0, concat_axis=0, tiled=True),
        lax.all_to_all(send_dy, "expert", split_axis=0, concat_axis=0, tiled=True),
        lax.all_to_all(send_gate, "expert", split_axis=0, concat_axis=0, tiled=True),
    )
    for bit in range(levels):
        got = partner((cur_x, cur_dy, cur_g), "expert", bit)
        lower = here // (1 << bit) % 2 == 0
        cur_x = jnp.where(
            lower,
            jnp.concatenate([cur_x, got[0]], axis=0),
            jnp.concatenate([got[0], cur_x], axis=0),
        )
        cur_dy = jnp.where(
            lower,
            jnp.concatenate([cur_dy, got[1]], axis=0),
            jnp.concatenate([got[1], cur_dy], axis=0),
        )
        cur_g = jnp.where(
            lower,
            jnp.concatenate([cur_g, got[2]], axis=0),
            jnp.concatenate([got[2], cur_g], axis=0),
        )
    rows_x, rows_dy, recv_gate = (cur_x, cur_dy, cur_g)
    pre_a = lax.dot_general(
        rows_x, full_gate, (((1,), (1,)), ((), ())), preferred_element_type=jnp.float32
    )
    pre_b = lax.dot_general(
        rows_x, full_up, (((1,), (1,)), ((), ())), preferred_element_type=jnp.float32
    )
    sig = jax.nn.sigmoid(pre_a)
    silu = pre_a * sig
    hidden = (silu * pre_b).astype(jnp.bfloat16)
    weight = recv_gate.astype(jnp.float32)
    probe = lax.dot_general(
        rows_dy, full_down, (((1,), (1,)), ((), ())), preferred_element_type=jnp.float32
    )
    share = jnp.sum(hidden.astype(jnp.float32) * probe, axis=1)
    scaled = (weight[:, None] * rows_dy.astype(jnp.float32)).astype(jnp.bfloat16)
    d_b = (weight[:, None] * probe * silu).astype(jnp.bfloat16)
    part_up = lax.dot_general(
        d_b, rows_x, (((0,), (0,)), ((), ())), preferred_element_type=jnp.float32
    )
    part_down = lax.dot_general(
        hidden, scaled, (((0,), (0,)), ((), ())), preferred_element_type=jnp.float32
    )
    folded = share.reshape(SPLIT, rows_all)
    for bit in reversed(range(levels)):
        half = folded.shape[0] // 2
        lower_half = folded[:half]
        upper_half = folded[half:]
        lower = here // (1 << bit) % 2 == 0
        keep = jnp.where(lower, lower_half, upper_half)
        away = jnp.where(lower, upper_half, lower_half)
        folded = keep + partner(away, "expert", bit)
    summed = lax.all_to_all(
        folded.reshape(rows_all), "expert", split_axis=0, concat_axis=0, tiled=True
    )
    gate_grad = jnp.dot(placed_f.T, summed, precision=lax.Precision.HIGHEST)
    sum_up, sum_down = (
        lax.psum_scatter(
            part_up.astype(jnp.bfloat16), "dp", scatter_dimension=1, tiled=True
        ).astype(jnp.float32),
        lax.psum_scatter(
            part_down.astype(jnp.bfloat16), "dp", scatter_dimension=1, tiled=True
        ).astype(jnp.float32),
    )
    return (
        sum_up.astype(jnp.bfloat16),
        sum_down.astype(jnp.bfloat16),
        gate_grad.reshape(tok_count, TOP),
    )


def solution(mesh):
    in_specs = (
        P(("expert", "dp"), None),
        P(("expert", "dp"), None),
        P(("expert", "dp"), None),
        P(("expert", "dp"), None),
        P("expert", "dp"),
        P("expert", "dp"),
        P("expert", "dp"),
    )
    out_specs = (P("expert", "dp"), P("expert", "dp"), P(("expert", "dp"), None))
    return jax.shard_map(shards, mesh=mesh, in_specs=in_specs, out_specs=out_specs, check_vma=False)
```
